32 devices in a mesh: row: 4 (over y, core), col: 8 (over z, x).
Axes of the slice: x: 2, y: 2, z: 4, core: 2. Of those that a mesh axis runs over, the one named last changes fastest.
Arguments:
- diag_block: float32 [1024, 1024], P('row')
- panel: bfloat16 [16, 1024, 1024], P('col', 'row'), may hold values from -1 to 1
- trailing: bfloat16 [8, 12, 1024, 1024], P('col', None, 'row'), may hold values from -6 to 6
- slot_rows: int32 [8, 12], replicated, may hold values from -1 to 15, as said below
- slot_cols: int32 [8, 12], replicated, may hold values from 0 to 1, as said below
Outputs:
- panel_factor: bfloat16 [16, 1024, 1024], P('col', 'row')
- updated: bfloat16 [8, 12, 1024, 1024], P('col', None, 'row')
The draws below stay inside these ranges and needn't reach their ends.
Inputs may be any that keep to these rules, and one draw needn't show every extreme that they name: Slot s of grid column c holds the tile at tile row slot_rows[c, s] and tile column 2 * c + slot_cols[c, s] of the trailing matrix, or nothing where slot_rows[c, s] is -1. Live slots come first in each column; the pairs of one column are distinct and lie on or below the diagonal (tile row at least tile column). Within one grid column, live slots whose tile rows a and a' have a // 2 == a' // 2 have a == a'. Every column holds at least one live slot, column 0 fills all 12 slots and column 4 holds exactly one. `slot_cols`: 0 in empty slots.
All inputs are finite; a program needn't handle non-finite values.
Results may differ from the reference program's by a relative error of at most 0.0019.
Values may be sent and summed in bfloat16 or wider, within the bound.
A program may use at most 128 MiB of HBM per device.

```python
import math
import jax
import jax.numpy as jnp
from jax import lax

TILE = 1024
PAN_COL = 2
SLOTS = 12
PANEL = 16
N_COL = 8


def compact_kernel(point_key):
    steps = jax.random.uniform(point_key, (TILE,), jnp.float32, 0.5, 1.5)
    points = jnp.cumsum(steps) / jnp.sum(steps)
    neighbours = min(64, TILE // 2)
    radius = neighbours / (2.0 * TILE)
    ratio = jnp.abs(points[:, None] - points[None, :]) / radius
    remain = jnp.maximum(1.0 - ratio, 0.0)
    squared = remain * remain
    return squared * squared * (4.0 * ratio + 1.0)


def draw_diag_block(key, part):
    first_key = jax.random.fold_in(jax.random.fold_in(key, 11), 0)
    second_key = jax.random.fold_in(jax.random.fold_in(key, 11), 1)
    fourth_key = jax.random.fold_in(jax.random.fold_in(key, 11), 3)
    basis = jax.random.normal(first_key, (TILE, TILE), jnp.float32) / math.sqrt(TILE)
    gram_part = 0.5 * jnp.dot(basis, basis.T, precision=lax.Precision.HIGHEST)
    extra_diag = jax.random.uniform(second_key, (TILE,), jnp.float32, 0.5, 1.5)
    matrix = compact_kernel(fourth_key) + gram_part + jnp.diag(extra_diag)
    return matrix


def slot_pattern(key):

    def one_column(col_index):
        column_key = jax.random.fold_in(jax.random.fold_in(key, 7), col_index)
        first_key, second_key, third_key = jax.random.split(column_key, 3)
        owners = jnp.arange(N_COL, dtype=jnp.int32)
        chosen_rows = owners * PAN_COL + jax.random.randint(third_key, (N_COL,), 0, PAN_COL, dtype=jnp.int32)
        candidate = jnp.arange(N_COL * PAN_COL, dtype=jnp.int32)
        owner_of = candidate // PAN_COL
        local_col = candidate % PAN_COL
        tile_row = chosen_rows[owner_of]
        allowed = (owner_of >= col_index) & (tile_row >= col_index * PAN_COL + local_col)
        scores = jax.random.randint(first_key, (N_COL * PAN_COL,), 0, 1 << 20, dtype=jnp.int32) * (N_COL * PAN_COL) + candidate
        scores = jnp.where(allowed, scores, (1 << 30) + candidate)
        ranked = jnp.argsort(scores, stable=True)[:SLOTS].astype(jnp.int32)
        available = jnp.sum(allowed.astype(jnp.int32))
        ceiling = jnp.minimum(available, SLOTS)
        live_count = jax.random.randint(second_key, (), 1, ceiling + 1, dtype=jnp.int32)
        live_count = jnp.where(col_index == 0, SLOTS, jnp.where(col_index == N_COL // 2, 1, live_count))
        live_mask = jnp.arange(SLOTS, dtype=jnp.int32) < live_count
        row_ids = jnp.where(live_mask, chosen_rows[ranked // PAN_COL], -1)
        col_ids = jnp.where(live_mask, ranked % PAN_COL, 0)
        return (row_ids.astype(jnp.int32), col_ids.astype(jnp.int32))
    return jax.vmap(one_column)(jnp.arange(N_COL, dtype=jnp.int32))


def draw_slot_rows(key, part):
    return slot_pattern(key)[0]


def draw_slot_cols(key, part):
    return slot_pattern(key)[1]


def steps_of(key, extent, shards, low, largest):
    def one(position, parts):
        steps = jax.random.uniform(jax.random.fold_in(jax.random.fold_in(key, 6), position), (parts,), jnp.float32, low / len(shards), largest / len(shards))
        return jnp.repeat(jnp.exp(steps), extent[position] // parts).reshape((-1,) + (1,) * (len(extent) - position - 1))

    level = one(*shards[0])
    for cut in shards[1:]:
        level = level * one(*cut)
    return level


def noise(key, dims, width, reach, shards=(), kind=jnp.bfloat16):
    entries = width * jax.random.normal(key, dims, jnp.float32)
    if shards:
        entries = entries * steps_of(key, dims, shards, -0.22, 0.18)
    return jnp.clip(entries, -reach, reach).astype(kind)


def setup_inputs(seed: int = 0) -> dict:
    key_of = jax.random.split(jax.random.key(seed), 6)
    diag_block = draw_diag_block(jax.random.fold_in(key_of[5], 71), 0)
    panel = noise(key_of[1], (PANEL, TILE, TILE), 0.18, 1.0, ((0, 8), (1, 4)))
    trailing = noise(key_of[2], (N_COL, SLOTS, TILE, TILE), 1.0, 6.0, ((0, 8), (2, 4)))
    slot_rows = draw_slot_rows(jax.random.fold_in(key_of[5], 71), 0)
    slot_cols = draw_slot_cols(jax.random.fold_in(key_of[5], 71), 0)
    return dict(diag_block=diag_block, panel=panel, trailing=trailing, slot_rows=slot_rows, slot_cols=slot_cols)


def reference(diag_block, panel, trailing, slot_rows, slot_cols):
    factor = jnp.linalg.cholesky(diag_block)
    stacked = panel.astype(jnp.float32).reshape(PANEL * TILE, TILE)
    solved = lax.linalg.triangular_solve(factor, stacked.T, left_side=True, lower=True)
    panel_factor = solved.T.reshape(PANEL, TILE, TILE).astype(jnp.bfloat16)
    widened = panel_factor.astype(jnp.float32)

    def one_column(packed):
        tile_block, row_ids, col_ids, col_index = packed
        live_mask = row_ids >= 0
        left_tiles = widened[jnp.maximum(row_ids, 0)]
        right_tiles = widened[col_index * PAN_COL + col_ids]
        update = jnp.einsum('sij,skj->sik', left_tiles, right_tiles, precision=lax.Precision.HIGHEST)
        previous = tile_block.astype(jnp.float32)
        lowered = jnp.where(live_mask[:, None, None], previous - update, previous)
        return lowered.astype(jnp.bfloat16)
    updated = lax.map(one_column, (trailing, slot_rows, slot_cols, jnp.arange(N_COL, dtype=jnp.int32)))
    return (panel_factor, updated)
```

```python
import functools
import jax
import jax.numpy as jnp
from jax import lax
from jax.experimental import pallas as pl
from jax.experimental.pallas import tpu as pltpu
from jax.sharding import PartitionSpec as P

BLOCK = 128
GROUP = 4
SUB = 8
LIMIT = 60 << 20


def split(x):
    high = x.astype(jnp.bfloat16)
    return high, (x - high.astype(jnp.float32)).astype(jnp.bfloat16)


def dot3(ah, al, bh, bl, dims):
    d = functools.partial(
        lax.dot_general, dimension_numbers=(dims, ((), ())), preferred_element_type=jnp.float32
    )
    return d(ah, bh) + (d(ah, bl) + d(al, bh))


def invert_factor(rows):
    rows = list(rows)
    lane = lax.broadcasted_iota(jnp.int32, (SUB, BLOCK), 1)
    sub = lax.broadcasted_iota(jnp.int32, (SUB, BLOCK), 0)
    lane1 = lane[:1]
    for c in range(0, BLOCK, GROUP):
        v0, s = divmod(c, SUB)
        last = s + GROUP == SUB
        strips = range(v0, len(rows))
        cols = [
            {i: jnp.broadcast_to(rows[i][:, c + j : c + j + 1], (SUB, BLOCK)) for i in strips}
            for j in range(GROUP)
        ]
        piv = [[cols[j][v0][s + i : s + i + 1, :] for j in range(i + 1)] for i in range(GROUP)]
        low = [[None] * GROUP for _ in range(GROUP)]
        inv = []
        for t in range(GROUP):
            for i in range(t, GROUP):
                low[i][t] = piv[i][t]
            for m in range(t):
                for i in range(t, GROUP):
                    low[i][t] = low[i][t] - low[i][m] * low[t][m]
            inv.append(lax.rsqrt(low[t][t]))
            for i in range(t + 1, GROUP):
                low[i][t] = low[i][t] * inv[t]
        ingroup1 = (lane1 >= c) & (lane1 < c + GROUP)
        solved = []
        for t in range(GROUP):
            x = rows[v0][s + t : s + t + 1, :]
            x = jnp.where(ingroup1, jnp.where(lane1 == c + t, 1.0, 0.0), x)
            for m in range(t):
                x = x - low[t][m] * solved[m]
            solved.append(x * inv[t])
        wide = [jnp.broadcast_to(x, (SUB, BLOCK)) for x in solved]
        ingroup = (lane >= c) & (lane < c + GROUP)
        for i in strips:
            if i == v0 and last:
                new = rows[i]
            else:
                mult = []
                new = jnp.where(ingroup, 0.0, rows[i])
                for t in range(GROUP):
                    y = cols[t][i]
                    for m in range(t):
                        y = y - mult[m] * low[t][m]
                    mult.append(y * inv[t])
                    new = new - mult[t] * wide[t]
            if i == v0:
                if not last:
                    new = jnp.where(sub >= s + GROUP, new, rows[i])
                for t in range(GROUP):
                    new = jnp.where(sub == s + t, wide[t], new)
            rows[i] = new
    return rows


def factor_kernel(diag_ref, high_ref, low_ref, work, row_high, row_low):
    n = diag_ref.shape[0]
    steps = n // BLOCK
    work[...] = diag_ref[...]
    row_id = lax.broadcasted_iota(jnp.int32, (BLOCK, BLOCK), 0)
    lane_id = lax.broadcasted_iota(jnp.int32, (BLOCK, BLOCK), 1)

    @pl.loop(0, steps)
    def _(k):
        here = pl.multiple_of(k * BLOCK, BLOCK)
        strips = [
            work[pl.ds(pl.multiple_of(here + i * SUB, SUB), SUB), pl.ds(here, BLOCK)]
            for i in range(BLOCK // SUB)
        ]
        inverse = jnp.concatenate(invert_factor(strips), axis=0)
        inverse = jnp.where(lane_id <= row_id, inverse, 0.0)
        ih, il = split(inverse)
        xh, xl = split(work[pl.ds(here, BLOCK), :])
        panel = dot3(ih, il, xh, xl, ((1,), (0,)))
        ph, plow = split(panel)
        work[pl.ds(here, BLOCK), :] = panel
        row_high[...] = ph
        row_low[...] = plow
        work[pl.ds(here, BLOCK), pl.ds(here, BLOCK)] = inverse
        row_high[:, pl.ds(here, BLOCK)] = ih
        row_low[:, pl.ds(here, BLOCK)] = il

        @pl.loop(k + 1, steps)
        def _(i):
            there = pl.multiple_of(i * BLOCK, BLOCK)
            lh = row_high[:, pl.ds(there, BLOCK)]
            ll = row_low[:, pl.ds(there, BLOCK)]
            work[pl.ds(there, BLOCK), pl.ds(here, BLOCK)] = jnp.zeros((BLOCK, BLOCK), jnp.float32)
            work[pl.ds(there, BLOCK), :] -= dot3(
                lh, ll, row_high[...], row_low[...], ((0,), (0,))
            )

    @pl.loop(0, steps)
    def _(k):
        here = pl.multiple_of(k * BLOCK, BLOCK)
        strip = work[pl.ds(here, BLOCK), :]
        r = lax.broadcasted_iota(jnp.int32, strip.shape, 0) + here
        c = lax.broadcasted_iota(jnp.int32, strip.shape, 1)
        h, l = split(jnp.where(c <= r, strip, 0.0))
        high_ref[pl.ds(here, BLOCK), :] = h
        low_ref[pl.ds(here, BLOCK), :] = l


def invert(diag):
    n = diag.shape[0]
    vmem = pl.BlockSpec(memory_space=pltpu.VMEM)
    return pl.pallas_call(
        factor_kernel,
        out_shape=[jax.ShapeDtypeStruct((n, n), jnp.bfloat16)] * 2,
        in_specs=[vmem],
        out_specs=[vmem, vmem],
        scratch_shapes=[
            pltpu.VMEM((n, n), jnp.float32),
            pltpu.VMEM((BLOCK, n), jnp.bfloat16),
            pltpu.VMEM((BLOCK, n), jnp.bfloat16),
        ],
        compiler_params=pltpu.CompilerParams(vmem_limit_bytes=LIMIT),
        cost_estimate=pl.CostEstimate(
            flops=60 * n**3, bytes_accessed=8 * n * n, transcendentals=n
        ),
        name="invert_factor",
    )(diag)


def solve_kernel(x_ref, high_ref, low_ref, out_ref):
    dims = (((1,), (1,)), ((), ()))
    x = x_ref[...]
    y = lax.dot_general(x, low_ref[...], dims, preferred_element_type=jnp.float32)
    y = y + lax.dot_general(x, high_ref[...], dims, preferred_element_type=jnp.float32)
    out_ref[...] = y.astype(out_ref.dtype)


def solve(x, high, low):
    m, n = x.shape
    rows = min(256, m)
    resident = pl.BlockSpec((n, n), lambda i: (0, 0), pipeline_mode=pl.Buffered(1))
    block = pl.BlockSpec((rows, n), lambda i: (i, 0))
    return pl.pallas_call(
        solve_kernel,
        grid=(m // rows,),
        out_shape=jax.ShapeDtypeStruct((m, n), jnp.bfloat16),
        in_specs=[block, resident, resident],
        out_specs=block,
        compiler_params=pltpu.CompilerParams(vmem_limit_bytes=LIMIT),
        name="solve_rows",
    )(x, high, low)


def slot_kernel(live_ref, left_id_ref, col_id_ref, left_ref, right_ref, trail_ref, out_ref):
    s = pl.program_id(0)

    @pl.when(live_ref[s] > 0)
    def _():
        product = lax.dot_general(
            left_ref[...],
            right_ref[...],
            (((1,), (1,)), ((), ())),
            preferred_element_type=jnp.float32,
        )
        out_ref[...] = (trail_ref[...].astype(jnp.float32) - product).astype(out_ref.dtype)

    @pl.when(live_ref[s] == 0)
    def _():
        out_ref[...] = trail_ref[...]


def apply_slots(live, left_ids, col_ids, slices, tiles, trailing):
    slots, rows, n = trailing.shape
    return pl.pallas_call(
        slot_kernel,
        out_shape=jax.ShapeDtypeStruct(trailing.shape, trailing.dtype),
        grid_spec=pltpu.PrefetchScalarGridSpec(
            num_scalar_prefetch=3,
            grid=(slots,),
            in_specs=[
                pl.BlockSpec((None, rows, n), lambda s, v, a, b: (a[s], 0, 0)),
                pl.BlockSpec((None, n, n), lambda s, v, a, b: (b[s], 0, 0)),
                pl.BlockSpec((None, rows, n), lambda s, v, a, b: (s, 0, 0)),
            ],
            out_specs=pl.BlockSpec((None, rows, n), lambda s, v, a, b: (s, 0, 0)),
        ),
        compiler_params=pltpu.CompilerParams(vmem_limit_bytes=LIMIT),
        name="apply_slots",
    )(live, left_ids, col_ids, slices, tiles, trailing)


def local(diag_block, panel, trailing, slot_rows, slot_cols):
    tile_count, row_count, n = panel.shape
    diag_full = lax.all_gather(diag_block, "row", axis=0, tiled=True)
    column_index = lax.axis_index("col")
    own_rows = lax.dynamic_index_in_dim(slot_rows, column_index, 0, keepdims=False)
    own_cols = lax.dynamic_index_in_dim(slot_cols, column_index, 0, keepdims=False)
    mine = (slot_rows >= 0) & (slot_rows // tile_count == column_index)
    local_pick = jnp.max(jnp.where(mine, slot_rows % tile_count, 0), axis=1)
    outgoing = jnp.broadcast_to(panel[0], (slot_rows.shape[0], row_count, n))
    for p in range(1, tile_count):
        outgoing = jnp.where((local_pick == p)[:, None, None], panel[p], outgoing)
    raw_slices = lax.all_to_all(outgoing, "col", split_axis=0, concat_axis=0, tiled=True)
    raw_tiles = lax.all_gather(panel, "row", axis=1, tiled=True)
    high, low = invert(diag_full)
    tiles = solve(raw_tiles.reshape(-1, n), high, low).reshape(raw_tiles.shape)
    slices = solve(raw_slices.reshape(-1, n), high, low).reshape(raw_slices.shape)
    panel_factor = lax.dynamic_slice_in_dim(
        tiles, lax.axis_index("row") * row_count, row_count, axis=1
    )
    live = (own_rows >= 0).astype(jnp.int32)
    left_ids = jnp.maximum(own_rows, 0) // tile_count
    updated = apply_slots(live, left_ids, own_cols, slices, tiles, trailing[0])
    return (panel_factor, updated[None])


def solution(mesh):
    return jax.shard_map(
        local,
        mesh=mesh,
        in_specs=(P("row", None), P("col", "row", None), P("col", None, "row", None), P(), P()),
        out_specs=(P("col", "row", None), P("col", None, "row", None)),
        check_vma=False,
    )
```

```python
import functools
import jax
import jax.numpy as jnp
from jax import lax
from jax.experimental import pallas as pl
from jax.experimental.pallas import tpu as pltpu
from jax.sharding import PartitionSpec as P

BLOCK = 128
GROUP = 4
SUB = 8
LIMIT = 60 << 20
WIDE = 256
CHUNK = 1024
OWNED = 1024


def split(x):
    high = x.astype(jnp.bfloat16)
    return high, (x - high.astype(jnp.float32)).astype(jnp.bfloat16)


def dot3(ah, al, bh, bl, dims):
    d = functools.partial(
        lax.dot_general, dimension_numbers=(dims, ((), ())), preferred_element_type=jnp.float32
    )
    return d(ah, bh) + (d(ah, bl) + d(al, bh))


def invert_factor(rows):
    rows = list(rows)
    lane = lax.broadcasted_iota(jnp.int32, (SUB, BLOCK), 1)
    sub = lax.broadcasted_iota(jnp.int32, (SUB, BLOCK), 0)
    lane1 = lane[:1]
    for c in range(0, BLOCK, GROUP):
        v0, s = divmod(c, SUB)
        last = s + GROUP == SUB
        strips = range(v0, len(rows))
        cols = [
            {i: jnp.broadcast_to(rows[i][:, c + j : c + j + 1], (SUB, BLOCK)) for i in strips}
            for j in range(GROUP)
        ]
        piv = [[cols[j][v0][s + i : s + i + 1, :] for j in range(i + 1)] for i in range(GROUP)]
        low = [[None] * GROUP for _ in range(GROUP)]
        inv = []
        for t in range(GROUP):
            for i in range(t, GROUP):
                low[i][t] = piv[i][t]
            for m in range(t):
                for i in range(t, GROUP):
                    low[i][t] = low[i][t] - low[i][m] * low[t][m]
            inv.append(lax.rsqrt(low[t][t]))
            for i in range(t + 1, GROUP):
                low[i][t] = low[i][t] * inv[t]
        ingroup1 = (lane1 >= c) & (lane1 < c + GROUP)
        solved = []
        for t in range(GROUP):
            x = rows[v0][s + t : s + t + 1, :]
            x = jnp.where(ingroup1, jnp.where(lane1 == c + t, 1.0, 0.0), x)
            for m in range(t):
                x = x - low[t][m] * solved[m]
            solved.append(x * inv[t])
        wide = [jnp.broadcast_to(x, (SUB, BLOCK)) for x in solved]
        ingroup = (lane >= c) & (lane < c + GROUP)
        for i in strips:
            if i == v0 and last:
                new = rows[i]
            else:
                mult = []
                new = jnp.where(ingroup, 0.0, rows[i])
                for t in range(GROUP):
                    y = cols[t][i]
                    for m in range(t):
                        y = y - mult[m] * low[t][m]
                    mult.append(y * inv[t])
                    new = new - mult[t] * wide[t]
            if i == v0:
                if not last:
                    new = jnp.where(sub >= s + GROUP, new, rows[i])
                for t in range(GROUP):
                    new = jnp.where(sub == s + t, wide[t], new)
            rows[i] = new
    return rows


def factor_kernel(diag_ref, high_ref, low_ref, work, row_high, row_low):
    n = diag_ref.shape[0]
    steps = n // BLOCK
    work[...] = diag_ref[...]
    row_id = lax.broadcasted_iota(jnp.int32, (BLOCK, BLOCK), 0)
    lane_id = lax.broadcasted_iota(jnp.int32, (BLOCK, BLOCK), 1)

    @pl.loop(0, steps)
    def _(k):
        here = pl.multiple_of(k * BLOCK, BLOCK)
        strips = [
            work[pl.ds(pl.multiple_of(here + i * SUB, SUB), SUB), pl.ds(here, BLOCK)]
            for i in range(BLOCK // SUB)
        ]
        inverse = jnp.concatenate(invert_factor(strips), axis=0)
        inverse = jnp.where(lane_id <= row_id, inverse, 0.0)
        ih, il = split(inverse)
        xh, xl = split(work[pl.ds(here, BLOCK), :])
        panel = dot3(ih, il, xh, xl, ((1,), (0,)))
        ph, plow = split(panel)
        work[pl.ds(here, BLOCK), :] = panel
        row_high[...] = ph
        row_low[...] = plow
        work[pl.ds(here, BLOCK), pl.ds(here, BLOCK)] = inverse
        row_high[:, pl.ds(here, BLOCK)] = ih
        row_low[:, pl.ds(here, BLOCK)] = il

        @pl.loop(k + 1, steps)
        def _(i):
            there = pl.multiple_of(i * BLOCK, BLOCK)
            lh = row_high[:, pl.ds(there, BLOCK)]
            ll = row_low[:, pl.ds(there, BLOCK)]
            work[pl.ds(there, BLOCK), pl.ds(here, BLOCK)] = jnp.zeros((BLOCK, BLOCK), jnp.float32)
            work[pl.ds(there, BLOCK), :] -= dot3(
                lh, ll, row_high[...], row_low[...], ((0,), (0,))
            )

    @pl.loop(0, steps)
    def _(k):
        here = pl.multiple_of(k * BLOCK, BLOCK)
        strip = work[pl.ds(here, BLOCK), :]
        r = lax.broadcasted_iota(jnp.int32, strip.shape, 0) + here
        c = lax.broadcasted_iota(jnp.int32, strip.shape, 1)
        h, l = split(jnp.where(c <= r, strip, 0.0))
        high_ref[pl.ds(here, BLOCK), :] = h
        low_ref[pl.ds(here, BLOCK), :] = l


def invert(diag):
    n = diag.shape[0]
    vmem = pl.BlockSpec(memory_space=pltpu.VMEM)
    return pl.pallas_call(
        factor_kernel,
        out_shape=[jax.ShapeDtypeStruct((n, n), jnp.bfloat16)] * 2,
        in_specs=[vmem],
        out_specs=[vmem, vmem],
        scratch_shapes=[
            pltpu.VMEM((n, n), jnp.float32),
            pltpu.VMEM((BLOCK, n), jnp.bfloat16),
            pltpu.VMEM((BLOCK, n), jnp.bfloat16),
        ],
        compiler_params=pltpu.CompilerParams(vmem_limit_bytes=LIMIT),
        cost_estimate=pl.CostEstimate(
            flops=60 * n**3, bytes_accessed=8 * n * n, transcendentals=n
        ),
        name="invert_factor",
    )(diag)


def solve_into(x, high_ref, low_ref, store):
    n = x.shape[1]
    dims = (((1,), (1,)), ((), ()))
    for j in range(0, n, WIDE):
        end = min(j + WIDE, n)
        y = lax.dot_general(
            x[:, :end], low_ref[j:end, :end], dims, preferred_element_type=jnp.float32
        ) + lax.dot_general(
            x[:, :end], high_ref[j:end, :end], dims, preferred_element_type=jnp.float32
        )
        store(slice(j, end), y.astype(jnp.bfloat16))


def finish_kernel(
    plan, place_ref, live_ref, left_id_ref, col_id_ref, wanted_ref,
    high_ref, low_ref, tile_ref, slice_ref, trail_ref,
    factor_ref, out_ref, tiles, slices,
):
    chunks, per_tile, chunk, owner_steps, owners = plan
    step = pl.program_id(0)
    row_count = factor_ref.shape[1]

    @pl.when(step < chunks)
    def _():
        tile = step // per_tile
        start = pl.multiple_of((step % per_tile) * chunk, chunk)

        def store(cols, y):
            tiles[tile, pl.ds(start, chunk), cols] = y

        solve_into(tile_ref[...], high_ref, low_ref, store)

    @pl.when((step >= chunks) & (step < chunks + owner_steps))
    def _():
        first = (step - chunks) * owners
        need = wanted_ref[first]
        for q in range(1, owners):
            need = need + wanted_ref[first + q]

        @pl.when(need > 0)
        def _():
            def store(cols, y):
                slices[pl.ds(first, owners), :, cols] = y.reshape(owners, row_count, -1)

            x = slice_ref[...].reshape(owners * row_count, -1)
            solve_into(x, high_ref, low_ref, store)

    @pl.when(step == chunks)
    def _():
        start = pl.multiple_of(place_ref[0] * row_count, row_count)
        factor_ref[...] = tiles[:, pl.ds(start, row_count), :]

    @pl.when(step >= chunks + owner_steps)
    def _():
        s = step - chunks - owner_steps

        @pl.when(live_ref[s] > 0)
        def _():
            product = lax.dot_general(
                slices[left_id_ref[s]],
                tiles[col_id_ref[s]],
                (((1,), (1,)), ((), ())),
                preferred_element_type=jnp.float32,
            )
            out_ref[...] = (trail_ref[...].astype(jnp.float32) - product).astype(out_ref.dtype)

        @pl.when(live_ref[s] == 0)
        def _():
            out_ref[...] = trail_ref[...]


def finish(place, live, left_ids, col_ids, wanted, high, low, raw_tiles, raw_slices, trailing):
    slots, row_count, n = trailing.shape
    tile_count = raw_tiles.shape[0]
    col_count = raw_slices.shape[0]
    chunk = min(CHUNK, n)
    per_tile = n // chunk
    chunks = tile_count * per_tile
    owners = max(1, min(col_count, OWNED // row_count))
    owner_steps = col_count // owners
    plan = (chunks, per_tile, chunk, owner_steps, owners)
    before = chunks + owner_steps
    resident = pl.BlockSpec((n, n), lambda i, *_: (0, 0), pipeline_mode=pl.Buffered(1))

    def tile_map(i, *_):
        i = jnp.minimum(i, chunks - 1)
        return (i // per_tile, i % per_tile, 0)

    def slice_map(i, *_):
        return (jnp.clip(i - chunks, 0, owner_steps - 1), 0, 0)

    def slot_map(i, *_):
        return (jnp.clip(i - before, 0, slots - 1), 0, 0)

    return pl.pallas_call(
        functools.partial(finish_kernel, plan),
        out_shape=[
            jax.ShapeDtypeStruct((tile_count, row_count, n), jnp.bfloat16),
            jax.ShapeDtypeStruct(trailing.shape, trailing.dtype),
        ],
        grid_spec=pltpu.PrefetchScalarGridSpec(
            num_scalar_prefetch=5,
            grid=(before + slots,),
            in_specs=[
                resident,
                resident,
                pl.BlockSpec((None, chunk, n), tile_map),
                pl.BlockSpec((owners, row_count, n), slice_map),
                pl.BlockSpec((None, row_count, n), slot_map),
            ],
            out_specs=[
                pl.BlockSpec((tile_count, row_count, n), lambda i, *_: (0, 0, 0)),
                pl.BlockSpec((None, row_count, n), slot_map),
            ],
            scratch_shapes=[
                pltpu.VMEM((tile_count, n, n), jnp.bfloat16),
                pltpu.VMEM((col_count, row_count, n), jnp.bfloat16),
            ],
        ),
        compiler_params=pltpu.CompilerParams(vmem_limit_bytes=LIMIT),
        name="finish",
    )(place, live, left_ids, col_ids, wanted, high, low, raw_tiles, raw_slices, trailing)


def local(diag_block, panel, trailing, slot_rows, slot_cols):
    tile_count, row_count, n = panel.shape
    diag_full = lax.all_gather(diag_block, "row", axis=0, tiled=True)
    column_index = lax.axis_index("col")
    own_rows = lax.dynamic_index_in_dim(slot_rows, column_index, 0, keepdims=False)
    own_cols = lax.dynamic_index_in_dim(slot_cols, column_index, 0, keepdims=False)
    mine = (slot_rows >= 0) & (slot_rows // tile_count == column_index)
    local_pick = jnp.max(jnp.where(mine, slot_rows % tile_count, 0), axis=1)
    outgoing = jnp.broadcast_to(panel[0], (slot_rows.shape[0], row_count, n))
    for p in range(1, tile_count):
        outgoing = jnp.where((local_pick == p)[:, None, None], panel[p], outgoing)
    raw_slices = lax.all_to_all(outgoing, "col", split_axis=0, concat_axis=0, tiled=True)
    raw_tiles = lax.all_gather(panel, "row", axis=1, tiled=True)
    high, low = invert(diag_full)
    live = (own_rows >= 0).astype(jnp.int32)
    left_ids = jnp.maximum(own_rows, 0) // tile_count
    owner = jnp.arange(slot_rows.shape[0], dtype=jnp.int32)
    wanted = jnp.any((left_ids[None, :] == owner[:, None]) & (own_rows >= 0)[None, :], axis=1)
    place = lax.axis_index("row").astype(jnp.int32).reshape(1)
    panel_factor, updated = finish(
        place, live, left_ids, own_cols, wanted.astype(jnp.int32),
        high, low, raw_tiles, raw_slices, trailing[0],
    )
    return (panel_factor, updated[None])


def solution(mesh):
    return jax.shard_map(
        local,
        mesh=mesh,
        in_specs=(P("row", None), P("col", "row", None), P("col", None, "row", None), P(), P()),
        out_specs=(P("col", "row", None), P("col", None, "row", None)),
        check_vma=False,
    )
```

```python
import functools
import jax
import jax.numpy as jnp
from jax import lax
from jax.experimental import pallas as pl
from jax.experimental.pallas import tpu as pltpu
from jax.sharding import PartitionSpec as P

BLOCK = 128
GROUP = 4
SUB = 8
LIMIT = 60 << 20
WIDE = 256
FACTOR_LIMIT = 40 << 20
OWNED = 1024


def split(x):
    high = x.astype(jnp.bfloat16)
    return high, (x - high.astype(jnp.float32)).astype(jnp.bfloat16)


def dot3(ah, al, bh, bl, dims):
    d = functools.partial(
        lax.dot_general, dimension_numbers=(dims, ((), ())), preferred_element_type=jnp.float32
    )
    return d(ah, bh) + (d(ah, bl) + d(al, bh))


def invert_factor(rows):
    rows = list(rows)
    lane = lax.broadcasted_iota(jnp.int32, (SUB, BLOCK), 1)
    sub = lax.broadcasted_iota(jnp.int32, (SUB, BLOCK), 0)
    lane1 = lane[:1]
    for c in range(0, BLOCK, GROUP):
        v0, s = divmod(c, SUB)
        last = s + GROUP == SUB
        strips = range(v0, len(rows))
        cols = [
            {i: jnp.broadcast_to(rows[i][:, c + j : c + j + 1], (SUB, BLOCK)) for i in strips}
            for j in range(GROUP)
        ]
        piv = [[cols[j][v0][s + i : s + i + 1, :] for j in range(i + 1)] for i in range(GROUP)]
        low = [[None] * GROUP for _ in range(GROUP)]
        inv = []
        for t in range(GROUP):
            for i in range(t, GROUP):
                low[i][t] = piv[i][t]
            for m in range(t):
                for i in range(t, GROUP):
                    low[i][t] = low[i][t] - low[i][m] * low[t][m]
            inv.append(lax.rsqrt(low[t][t]))
            for i in range(t + 1, GROUP):
                low[i][t] = low[i][t] * inv[t]
        ingroup1 = (lane1 >= c) & (lane1 < c + GROUP)
        solved = []
        for t in range(GROUP):
            x = rows[v0][s + t : s + t + 1, :]
            x = jnp.where(ingroup1, jnp.where(lane1 == c + t, 1.0, 0.0), x)
            for m in range(t):
                x = x - low[t][m] * solved[m]
            solved.append(x * inv[t])
        wide = [jnp.broadcast_to(x, (SUB, BLOCK)) for x in solved]
        ingroup = (lane >= c) & (lane < c + GROUP)
        for i in strips:
            if i == v0 and last:
                new = rows[i]
            else:
                mult = []
                new = jnp.where(ingroup, 0.0, rows[i])
                for t in range(GROUP):
                    y = cols[t][i]
                    for m in range(t):
                        y = y - mult[m] * low[t][m]
                    mult.append(y * inv[t])
                    new = new - mult[t] * wide[t]
            if i == v0:
                if not last:
                    new = jnp.where(sub >= s + GROUP, new, rows[i])
                for t in range(GROUP):
                    new = jnp.where(sub == s + t, wide[t], new)
            rows[i] = new
    return rows


def eliminate(work, row_high, row_low):
    n = work.shape[0]
    steps = n // BLOCK
    row_id = lax.broadcasted_iota(jnp.int32, (BLOCK, BLOCK), 0)
    lane_id = lax.broadcasted_iota(jnp.int32, (BLOCK, BLOCK), 1)

    @pl.loop(0, steps)
    def _(k):
        here = pl.multiple_of(k * BLOCK, BLOCK)
        strips = [
            work[pl.ds(pl.multiple_of(here + i * SUB, SUB), SUB), pl.ds(here, BLOCK)]
            for i in range(BLOCK // SUB)
        ]
        inverse = jnp.concatenate(invert_factor(strips), axis=0)
        inverse = jnp.where(lane_id <= row_id, inverse, 0.0)
        ih, il = split(inverse)
        xh, xl = split(work[pl.ds(here, BLOCK), :])
        panel = dot3(ih, il, xh, xl, ((1,), (0,)))
        ph, plow = split(panel)
        work[pl.ds(here, BLOCK), :] = panel
        row_high[...] = ph
        row_low[...] = plow
        work[pl.ds(here, BLOCK), pl.ds(here, BLOCK)] = inverse
        row_high[:, pl.ds(here, BLOCK)] = ih
        row_low[:, pl.ds(here, BLOCK)] = il

        @pl.loop(k + 1, steps)
        def _(i):
            there = pl.multiple_of(i * BLOCK, BLOCK)
            lh = row_high[:, pl.ds(there, BLOCK)]
            ll = row_low[:, pl.ds(there, BLOCK)]
            work[pl.ds(there, BLOCK), pl.ds(here, BLOCK)] = jnp.zeros((BLOCK, BLOCK), jnp.float32)
            work[pl.ds(there, BLOCK), :] -= dot3(
                lh, ll, row_high[...], row_low[...], ((0,), (0,))
            )


def lower(work):
    r = lax.broadcasted_iota(jnp.int32, work.shape, 0)
    c = lax.broadcasted_iota(jnp.int32, work.shape, 1)
    return split(jnp.where(c <= r, work[...], 0.0))


def put_rows(place_ref, pieces, target, first, count):
    pairs = len(pieces) // 2
    rows = pieces[0].shape[0]
    y, core = place_ref[0] // 2, place_ref[0] % 2
    for s in range(pairs):
        source = (y + pairs - s) % pairs - first
        for d in range(2):
            start = pl.multiple_of((source * 2 + (core + d) % 2) * rows, rows)

            @pl.when((source >= 0) & (source < count))
            def _():
                target[pl.ds(start, rows), :] = pieces[2 * s + d][...]


def top_kernel(count, place_ref, *refs):
    pieces, (high_ref, low_ref, work, row_high, row_low) = refs[:-5], refs[-5:]
    put_rows(place_ref, pieces, work, 0, count)
    eliminate(work, row_high, row_low)
    h, l = lower(work)
    high_ref[...] = h
    low_ref[...] = l


def bottom_kernel(first, count, place_ref, th_ref, tl_ref, *refs):
    pieces, (high_ref, low_ref, rows_ref, work, row_high, row_low) = refs[:-6], refs[-6:]
    m = work.shape[0]
    put_rows(place_ref, pieces, rows_ref, first, count)
    th, tl = th_ref[...], tl_ref[...]
    ah, al = split(rows_ref[:, :m])
    lh, ll = split(dot3(ah, al, th, tl, ((1,), (1,))))
    work[...] = rows_ref[:, m:] - dot3(lh, ll, lh, ll, ((1,), (1,)))
    bh, bl = split(dot3(lh, ll, th, tl, ((1,), (0,))))
    eliminate(work, row_high, row_low)
    h, l = lower(work)
    high_ref[m:, m:] = h
    low_ref[m:, m:] = l
    ch, cl = split(-dot3(h, l, bh, bl, ((1,), (0,))))
    high_ref[m:, :m] = ch
    low_ref[m:, :m] = cl
    zero = jnp.zeros((m, m), jnp.bfloat16)
    high_ref[:m, :m] = th
    low_ref[:m, :m] = tl
    high_ref[:m, m:] = zero
    low_ref[:m, m:] = zero


def factor_call(kernel, place, operands, n, half, extra, name):
    vmem = pl.BlockSpec(memory_space=pltpu.VMEM)
    return pl.pallas_call(
        kernel,
        out_shape=[jax.ShapeDtypeStruct((n, n), jnp.bfloat16)] * 2,
        in_specs=[pl.BlockSpec(memory_space=pltpu.SMEM)] + [vmem] * len(operands),
        out_specs=[vmem, vmem],
        scratch_shapes=extra
        + [
            pltpu.VMEM((half, half), jnp.float32),
            pltpu.VMEM((BLOCK, half), jnp.bfloat16),
            pltpu.VMEM((BLOCK, half), jnp.bfloat16),
        ],
        compiler_params=pltpu.CompilerParams(vmem_limit_bytes=FACTOR_LIMIT),
        cost_estimate=pl.CostEstimate(
            flops=240 * half**3, bytes_accessed=8 * n * n, transcendentals=n
        ),
        name=name,
    )(place, *operands)


def spread(block, pairs, sources):
    pieces = []
    for s in range(pairs):
        moved = block
        if s:
            route = [(2 * y + c, 2 * ((y + s) % pairs) + c) for y in sources for c in range(2)]
            moved = lax.ppermute(block, "row", route)
        owners = [(y + s) % pairs for y in sources]
        swap = [(2 * y + c, 2 * y + 1 - c) for y in owners for c in range(2)]
        pieces += [moved, lax.ppermute(moved, "row", swap)]
    return pieces


def solve_into(x, high_ref, low_ref, store):
    n = x.shape[1]
    dims = (((1,), (1,)), ((), ()))
    for j in range(0, n, WIDE):
        end = min(j + WIDE, n)
        y = lax.dot_general(
            x[:, :end], low_ref[j:end, :end], dims, preferred_element_type=jnp.float32
        ) + lax.dot_general(
            x[:, :end], high_ref[j:end, :end], dims, preferred_element_type=jnp.float32
        )
        store(slice(j, end), y.astype(jnp.bfloat16))


def finish_kernel(
    plan, place_ref, live_ref, left_id_ref, col_id_ref, wanted_ref,
    high_ref, low_ref, *refs,
):
    pieces, (slice_ref, trail_ref, factor_ref, out_ref, tiles, slices) = refs[:-6], refs[-6:]
    chunks, owner_steps, owners = plan
    step = pl.program_id(0)
    row_count = factor_ref.shape[1]

    @pl.when(step < chunks)
    def _():
        pairs = len(pieces) // 2
        y, core = place_ref[0] // 2, place_ref[0] % 2
        starts = [
            pl.multiple_of(
                ((y + pairs - s) % pairs * 2 + (core + d) % 2) * row_count, row_count
            )
            for s in range(pairs)
            for d in range(2)
        ]

        def store(cols, out):
            for i, start in enumerate(starts):
                tiles[step, pl.ds(start, row_count), cols] = out[
                    i * row_count : (i + 1) * row_count
                ]

        solve_into(
            jnp.concatenate([piece[...] for piece in pieces], axis=0), high_ref, low_ref, store
        )

    @pl.when((step >= chunks) & (step < chunks + owner_steps))
    def _():
        first = (step - chunks) * owners
        need = wanted_ref[first]
        for q in range(1, owners):
            need = need + wanted_ref[first + q]

        @pl.when(need > 0)
        def _():
            def store(cols, y):
                slices[pl.ds(first, owners), :, cols] = y.reshape(owners, row_count, -1)

            x = slice_ref[...].reshape(owners * row_count, -1)
            solve_into(x, high_ref, low_ref, store)

    @pl.when(step == chunks)
    def _():
        start = pl.multiple_of(place_ref[0] * row_count, row_count)
        factor_ref[...] = tiles[:, pl.ds(start, row_count), :]

    @pl.when(step >= chunks + owner_steps)
    def _():
        s = step - chunks - owner_steps

        @pl.when(live_ref[s] > 0)
        def _():
            product = lax.dot_general(
                slices[left_id_ref[s]],
                tiles[col_id_ref[s]],
                (((1,), (1,)), ((), ())),
                preferred_element_type=jnp.float32,
            )
            out_ref[...] = (trail_ref[...].astype(jnp.float32) - product).astype(out_ref.dtype)

        @pl.when(live_ref[s] == 0)
        def _():
            out_ref[...] = trail_ref[...]


def finish(place, live, left_ids, col_ids, wanted, high, low, pieces, raw_slices, trailing):
    slots, row_count, n = trailing.shape
    tile_count = pieces[0].shape[0]
    col_count = raw_slices.shape[0]
    chunks = tile_count
    owners = max(1, min(col_count, OWNED // row_count))
    owner_steps = col_count // owners
    plan = (chunks, owner_steps, owners)
    before = chunks + owner_steps
    resident = pl.BlockSpec((n, n), lambda i, *_: (0, 0), pipeline_mode=pl.Buffered(1))

    def tile_map(i, *_):
        return (jnp.minimum(i, chunks - 1), 0, 0)

    def slice_map(i, *_):
        return (jnp.clip(i - chunks, 0, owner_steps - 1), 0, 0)

    def slot_map(i, *_):
        return (jnp.clip(i - before, 0, slots - 1), 0, 0)

    return pl.pallas_call(
        functools.partial(finish_kernel, plan),
        out_shape=[
            jax.ShapeDtypeStruct((tile_count, row_count, n), jnp.bfloat16),
            jax.ShapeDtypeStruct(trailing.shape, trailing.dtype),
        ],
        grid_spec=pltpu.PrefetchScalarGridSpec(
            num_scalar_prefetch=5,
            grid=(before + slots,),
            in_specs=[
                resident,
                resident,
                *[pl.BlockSpec((None, row_count, n), tile_map) for _ in pieces],
                pl.BlockSpec((owners, row_count, n), slice_map),
                pl.BlockSpec((None, row_count, n), slot_map),
            ],
            out_specs=[
                pl.BlockSpec((tile_count, row_count, n), lambda i, *_: (0, 0, 0)),
                pl.BlockSpec((None, row_count, n), slot_map),
            ],
            scratch_shapes=[
                pltpu.VMEM((tile_count, n, n), jnp.bfloat16),
                pltpu.VMEM((col_count, row_count, n), jnp.bfloat16),
            ],
        ),
        compiler_params=pltpu.CompilerParams(vmem_limit_bytes=LIMIT),
        name="finish",
    )(place, live, left_ids, col_ids, wanted, high, low, *pieces, raw_slices, trailing)


def local(diag_block, panel, trailing, slot_rows, slot_cols):
    tile_count, row_count, n = panel.shape
    half = n // 2
    pairs = lax.axis_size("row") // 2
    cut = pairs // 2
    place = lax.axis_index("row").astype(jnp.int32).reshape(1)
    top_rows = spread(diag_block[:, :half], pairs, range(cut))
    bottom_rows = spread(diag_block, pairs, range(cut, pairs))
    column_index = lax.axis_index("col")
    own_rows = lax.dynamic_index_in_dim(slot_rows, column_index, 0, keepdims=False)
    own_cols = lax.dynamic_index_in_dim(slot_cols, column_index, 0, keepdims=False)
    mine = (slot_rows >= 0) & (slot_rows // tile_count == column_index)
    local_pick = jnp.max(jnp.where(mine, slot_rows % tile_count, 0), axis=1)
    outgoing = jnp.broadcast_to(panel[0], (slot_rows.shape[0], row_count, n))
    for p in range(1, tile_count):
        outgoing = jnp.where((local_pick == p)[:, None, None], panel[p], outgoing)
    raw_slices = lax.all_to_all(outgoing, "col", split_axis=0, concat_axis=0, tiled=True)
    pieces = spread(panel, pairs, range(pairs))
    top = factor_call(
        functools.partial(top_kernel, cut), place, top_rows, half, half, [], "factor_top"
    )
    high, low = factor_call(
        functools.partial(bottom_kernel, cut, pairs - cut),
        place,
        [*top, *bottom_rows],
        n,
        half,
        [pltpu.VMEM((half, n), jnp.float32)],
        "factor_bottom",
    )
    live = (own_rows >= 0).astype(jnp.int32)
    left_ids = jnp.maximum(own_rows, 0) // tile_count
    owner = jnp.arange(slot_rows.shape[0], dtype=jnp.int32)
    wanted = jnp.any((left_ids[None, :] == owner[:, None]) & (own_rows >= 0)[None, :], axis=1)
    panel_factor, updated = finish(
        place, live, left_ids, own_cols, wanted.astype(jnp.int32),
        high, low, pieces, raw_slices, trailing[0],
    )
    return (panel_factor, updated[None])


def solution(mesh):
    return jax.shard_map(
        local,
        mesh=mesh,
        in_specs=(P("row", None), P("col", "row", None), P("col", None, "row", None), P(), P()),
        out_specs=(P("col", "row", None), P("col", None, "row", None)),
        check_vma=False,
    )
```

```python
import functools
import jax
import jax.numpy as jnp
from jax import lax
from jax.experimental import pallas as pl
from jax.experimental.pallas import tpu as pltpu
from jax.sharding import PartitionSpec as P

BLOCK = 128
GROUP = 4
SUB = 8
LIMIT = 60 << 20
WIDE = 256
FACTOR_LIMIT = 40 << 20
OWNED = 1024


def split(x):
    high = x.astype(jnp.bfloat16)
    return high, (x - high.astype(jnp.float32)).astype(jnp.bfloat16)


def dot3(ah, al, bh, bl, dims):
    d = functools.partial(
        lax.dot_general, dimension_numbers=(dims, ((), ())), preferred_element_type=jnp.float32
    )
    return d(ah, bh) + (d(ah, bl) + d(al, bh))


def invert_factor(rows):
    rows = list(rows)
    lane = lax.broadcasted_iota(jnp.int32, (SUB, BLOCK), 1)
    sub = lax.broadcasted_iota(jnp.int32, (SUB, BLOCK), 0)
    lane1 = lane[:1]
    for c in range(0, BLOCK, GROUP):
        v0, s = divmod(c, SUB)
        last = s + GROUP == SUB
        strips = range(v0, len(rows))
        cols = [
            {i: jnp.broadcast_to(rows[i][:, c + j : c + j + 1], (SUB, BLOCK)) for i in strips}
            for j in range(GROUP)
        ]
        piv = [[cols[j][v0][s + i : s + i + 1, :] for j in range(i + 1)] for i in range(GROUP)]
        low = [[None] * GROUP for _ in range(GROUP)]
        inv = []
        for t in range(GROUP):
            for i in range(t, GROUP):
                low[i][t] = piv[i][t]
            for m in range(t):
                for i in range(t, GROUP):
                    low[i][t] = low[i][t] - low[i][m] * low[t][m]
            inv.append(lax.rsqrt(low[t][t]))
            for i in range(t + 1, GROUP):
                low[i][t] = low[i][t] * inv[t]
        ingroup1 = (lane1 >= c) & (lane1 < c + GROUP)
        solved = []
        for t in range(GROUP):
            x = rows[v0][s + t : s + t + 1, :]
            x = jnp.where(ingroup1, jnp.where(lane1 == c + t, 1.0, 0.0), x)
            for m in range(t):
                x = x - low[t][m] * solved[m]
            solved.append(x * inv[t])
        wide = [jnp.broadcast_to(x, (SUB, BLOCK)) for x in solved]
        ingroup = (lane >= c) & (lane < c + GROUP)
        for i in strips:
            if i == v0 and last:
                new = rows[i]
            else:
                mult = []
                new = jnp.where(ingroup, 0.0, rows[i])
                for t in range(GROUP):
                    y = cols[t][i]
                    for m in range(t):
                        y = y - mult[m] * low[t][m]
                    mult.append(y * inv[t])
                    new = new - mult[t] * wide[t]
            if i == v0:
                if not last:
                    new = jnp.where(sub >= s + GROUP, new, rows[i])
                for t in range(GROUP):
                    new = jnp.where(sub == s + t, wide[t], new)
            rows[i] = new
    return rows


def eliminate(work, row_high, row_low):
    n = work.shape[0]
    steps = n // BLOCK
    row_id = lax.broadcasted_iota(jnp.int32, (BLOCK, BLOCK), 0)
    lane_id = lax.broadcasted_iota(jnp.int32, (BLOCK, BLOCK), 1)

    @pl.loop(0, steps)
    def _(k):
        here = pl.multiple_of(k * BLOCK, BLOCK)
        strips = [
            work[pl.ds(pl.multiple_of(here + i * SUB, SUB), SUB), pl.ds(here, BLOCK)]
            for i in range(BLOCK // SUB)
        ]
        inverse = jnp.concatenate(invert_factor(strips), axis=0)
        inverse = jnp.where(lane_id <= row_id, inverse, 0.0)
        ih, il = split(inverse)
        xh, xl = split(work[pl.ds(here, BLOCK), :])
        panel = dot3(ih, il, xh, xl, ((1,), (0,)))
        ph, plow = split(panel)
        work[pl.ds(here, BLOCK), :] = panel
        row_high[...] = ph
        row_low[...] = plow
        work[pl.ds(here, BLOCK), pl.ds(here, BLOCK)] = inverse
        row_high[:, pl.ds(here, BLOCK)] = ih
        row_low[:, pl.ds(here, BLOCK)] = il

        @pl.loop(k + 1, steps)
        def _(i):
            there = pl.multiple_of(i * BLOCK, BLOCK)
            lh = row_high[:, pl.ds(there, BLOCK)]
            ll = row_low[:, pl.ds(there, BLOCK)]
            work[pl.ds(there, BLOCK), pl.ds(here, BLOCK)] = jnp.zeros((BLOCK, BLOCK), jnp.float32)
            work[pl.ds(there, BLOCK), :] -= dot3(
                lh, ll, row_high[...], row_low[...], ((0,), (0,))
            )


def lower(work):
    r = lax.broadcasted_iota(jnp.int32, work.shape, 0)
    c = lax.broadcasted_iota(jnp.int32, work.shape, 1)
    return split(jnp.where(c <= r, work[...], 0.0))


def put_rows(place_ref, pieces, target, first, count):
    pairs = len(pieces) // 2
    rows = pieces[0].shape[0]
    y, core = place_ref[0] // 2, place_ref[0] % 2
    for s in range(pairs):
        source = (y + pairs - s) % pairs - first
        for d in range(2):
            start = pl.multiple_of((source * 2 + (core + d) % 2) * rows, rows)

            @pl.when((source >= 0) & (source < count))
            def _():
                target[pl.ds(start, rows), :] = pieces[2 * s + d][...]


def top_kernel(count, place_ref, *refs):
    pieces, (high_ref, low_ref, work, row_high, row_low) = refs[:-5], refs[-5:]
    put_rows(place_ref, pieces, work, 0, count)
    eliminate(work, row_high, row_low)
    h, l = lower(work)
    high_ref[...] = h
    low_ref[...] = l


def bottom_kernel(first, count, place_ref, th_ref, tl_ref, *refs):
    pieces, (high_ref, low_ref, rows_ref, work, row_high, row_low) = refs[:-6], refs[-6:]
    m = work.shape[0]
    put_rows(place_ref, pieces, rows_ref, first, count)
    th, tl = th_ref[...], tl_ref[...]
    ah, al = split(rows_ref[:, :m])
    lh, ll = split(dot3(ah, al, th, tl, ((1,), (1,))))
    work[...] = rows_ref[:, m:] - dot3(lh, ll, lh, ll, ((1,), (1,)))
    bh, bl = split(dot3(lh, ll, th, tl, ((1,), (0,))))
    eliminate(work, row_high, row_low)
    h, l = lower(work)
    high_ref[m:, m:] = h
    low_ref[m:, m:] = l
    ch, cl = split(-dot3(h, l, bh, bl, ((1,), (0,))))
    high_ref[m:, :m] = ch
    low_ref[m:, :m] = cl
    zero = jnp.zeros((m, m), jnp.bfloat16)
    high_ref[:m, :m] = th
    low_ref[:m, :m] = tl
    high_ref[:m, m:] = zero
    low_ref[:m, m:] = zero


def factor_call(kernel, place, operands, n, half, extra, name):
    vmem = pl.BlockSpec(memory_space=pltpu.VMEM)
    return pl.pallas_call(
        kernel,
        out_shape=[jax.ShapeDtypeStruct((n, n), jnp.bfloat16)] * 2,
        in_specs=[pl.BlockSpec(memory_space=pltpu.SMEM)] + [vmem] * len(operands),
        out_specs=[vmem, vmem],
        scratch_shapes=extra
        + [
            pltpu.VMEM((half, half), jnp.float32),
            pltpu.VMEM((BLOCK, half), jnp.bfloat16),
            pltpu.VMEM((BLOCK, half), jnp.bfloat16),
        ],
        compiler_params=pltpu.CompilerParams(vmem_limit_bytes=FACTOR_LIMIT),
        cost_estimate=pl.CostEstimate(
            flops=240 * half**3, bytes_accessed=8 * n * n, transcendentals=n
        ),
        name=name,
    )(place, *operands)


def across(block, pairs, sources):
    moved = [block]
    for s in range(1, pairs):
        route = [(2 * y + c, 2 * ((y + s) % pairs) + c) for y in sources for c in range(2)]
        moved.append(lax.ppermute(block, "row", route))
    return moved


def between(moved, pairs, sources, after=None):
    if after is not None:
        late, after = lax.optimization_barrier((moved[1:], after))
        moved = [moved[0], *late]
    pieces = []
    for s, block in enumerate(moved):
        owners = [(y + s) % pairs for y in sources]
        swap = [(2 * y + c, 2 * y + 1 - c) for y in owners for c in range(2)]
        pieces += [block, lax.ppermute(block, "row", swap)]
    return pieces, after


def solve_into(x, high_ref, low_ref, store):
    n = x.shape[1]
    dims = (((1,), (1,)), ((), ()))
    for j in range(0, n, WIDE):
        end = min(j + WIDE, n)
        y = lax.dot_general(
            x[:, :end], low_ref[j:end, :end], dims, preferred_element_type=jnp.float32
        ) + lax.dot_general(
            x[:, :end], high_ref[j:end, :end], dims, preferred_element_type=jnp.float32
        )
        store(slice(j, end), y.astype(jnp.bfloat16))


def finish_kernel(
    plan, place_ref, live_ref, left_id_ref, col_id_ref, wanted_ref,
    high_ref, low_ref, *refs,
):
    pieces, (slice_ref, trail_ref, factor_ref, out_ref, tiles, slices) = refs[:-6], refs[-6:]
    chunks, owner_steps, owners = plan
    step = pl.program_id(0)
    row_count = factor_ref.shape[1]

    @pl.when(step < chunks)
    def _():
        pairs = len(pieces) // 2
        y, core = place_ref[0] // 2, place_ref[0] % 2
        starts = [
            pl.multiple_of(
                ((y + pairs - s) % pairs * 2 + (core + d) % 2) * row_count, row_count
            )
            for s in range(pairs)
            for d in range(2)
        ]

        def store(cols, out):
            for i, start in enumerate(starts):
                tiles[step, pl.ds(start, row_count), cols] = out[
                    i * row_count : (i + 1) * row_count
                ]

        solve_into(
            jnp.concatenate([piece[...] for piece in pieces], axis=0), high_ref, low_ref, store
        )

    @pl.when((step >= chunks) & (step < chunks + owner_steps))
    def _():
        first = (step - chunks) * owners
        need = wanted_ref[first]
        for q in range(1, owners):
            need = need + wanted_ref[first + q]

        @pl.when(need > 0)
        def _():
            def store(cols, y):
                slices[pl.ds(first, owners), :, cols] = y.reshape(owners, row_count, -1)

            x = slice_ref[...].reshape(owners * row_count, -1)
            solve_into(x, high_ref, low_ref, store)

    @pl.when(step == chunks)
    def _():
        start = pl.multiple_of(place_ref[0] * row_count, row_count)
        factor_ref[...] = tiles[:, pl.ds(start, row_count), :]

    @pl.when(step >= chunks + owner_steps)
    def _():
        s = step - chunks - owner_steps

        @pl.when(live_ref[s] > 0)
        def _():
            product = lax.dot_general(
                slices[left_id_ref[s]],
                tiles[col_id_ref[s]],
                (((1,), (1,)), ((), ())),
                preferred_element_type=jnp.float32,
            )
            out_ref[...] = (trail_ref[...].astype(jnp.float32) - product).astype(out_ref.dtype)

        @pl.when(live_ref[s] == 0)
        def _():
            out_ref[...] = trail_ref[...]


def finish(place, live, left_ids, col_ids, wanted, high, low, pieces, raw_slices, trailing):
    slots, row_count, n = trailing.shape
    tile_count = pieces[0].shape[0]
    col_count = raw_slices.shape[0]
    chunks = tile_count
    owners = max(1, min(col_count, OWNED // row_count))
    owner_steps = col_count // owners
    plan = (chunks, owner_steps, owners)
    before = chunks + owner_steps
    resident = pl.BlockSpec((n, n), lambda i, *_: (0, 0), pipeline_mode=pl.Buffered(1))

    def tile_map(i, *_):
        return (jnp.minimum(i, chunks - 1), 0, 0)

    def slice_map(i, *_):
        return (jnp.clip(i - chunks, 0, owner_steps - 1), 0, 0)

    def slot_map(i, *_):
        return (jnp.clip(i - before, 0, slots - 1), 0, 0)

    return pl.pallas_call(
        functools.partial(finish_kernel, plan),
        out_shape=[
            jax.ShapeDtypeStruct((tile_count, row_count, n), jnp.bfloat16),
            jax.ShapeDtypeStruct(trailing.shape, trailing.dtype),
        ],
        grid_spec=pltpu.PrefetchScalarGridSpec(
            num_scalar_prefetch=5,
            grid=(before + slots,),
            in_specs=[
                resident,
                resident,
                *[pl.BlockSpec((None, row_count, n), tile_map) for _ in pieces],
                pl.BlockSpec((owners, row_count, n), slice_map),
                pl.BlockSpec((None, row_count, n), slot_map),
            ],
            out_specs=[
                pl.BlockSpec((tile_count, row_count, n), lambda i, *_: (0, 0, 0)),
                pl.BlockSpec((None, row_count, n), slot_map),
            ],
            scratch_shapes=[
                pltpu.VMEM((tile_count, n, n), jnp.bfloat16),
                pltpu.VMEM((col_count, row_count, n), jnp.bfloat16),
            ],
        ),
        compiler_params=pltpu.CompilerParams(vmem_limit_bytes=LIMIT),
        name="finish",
    )(place, live, left_ids, col_ids, wanted, high, low, *pieces, raw_slices, trailing)


def local(diag_block, panel, trailing, slot_rows, slot_cols):
    tile_count, row_count, n = panel.shape
    half = n // 2
    pairs = lax.axis_size("row") // 2
    cut = pairs // 2
    place = lax.axis_index("row").astype(jnp.int32).reshape(1)
    top_rows, _ = between(across(diag_block[:, :half], pairs, range(cut)), pairs, range(cut))
    bottom_moved = across(diag_block, pairs, range(cut, pairs))
    column_index = lax.axis_index("col")
    own_rows = lax.dynamic_index_in_dim(slot_rows, column_index, 0, keepdims=False)
    own_cols = lax.dynamic_index_in_dim(slot_cols, column_index, 0, keepdims=False)
    mine = (slot_rows >= 0) & (slot_rows // tile_count == column_index)
    local_pick = jnp.max(jnp.where(mine, slot_rows % tile_count, 0), axis=1)
    outgoing = jnp.broadcast_to(panel[0], (slot_rows.shape[0], row_count, n))
    for p in range(1, tile_count):
        outgoing = jnp.where((local_pick == p)[:, None, None], panel[p], outgoing)
    raw_slices = lax.all_to_all(outgoing, "col", split_axis=0, concat_axis=0, tiled=True)
    panel_moved = across(panel, pairs, range(pairs))
    top = factor_call(
        functools.partial(top_kernel, cut), place, top_rows, half, half, [], "factor_top"
    )
    bottom_rows, top = between(bottom_moved, pairs, range(cut, pairs), top)
    inverse = factor_call(
        functools.partial(bottom_kernel, cut, pairs - cut),
        place,
        [*top, *bottom_rows],
        n,
        half,
        [pltpu.VMEM((half, n), jnp.float32)],
        "factor_bottom",
    )
    pieces, (high, low) = between(panel_moved, pairs, range(pairs), inverse)
    live = (own_rows >= 0).astype(jnp.int32)
    left_ids = jnp.maximum(own_rows, 0) // tile_count
    owner = jnp.arange(slot_rows.shape[0], dtype=jnp.int32)
    wanted = jnp.any((left_ids[None, :] == owner[:, None]) & (own_rows >= 0)[None, :], axis=1)
    panel_factor, updated = finish(
        place, live, left_ids, own_cols, wanted.astype(jnp.int32),
        high, low, pieces, raw_slices, trailing[0],
    )
    return (panel_factor, updated[None])


def solution(mesh):
    return jax.shard_map(
        local,
        mesh=mesh,
        in_specs=(P("row", None), P("col", "row", None), P("col", None, "row", None), P(), P()),
        out_specs=(P("col", "row", None), P("col", None, "row", None)),
        check_vma=False,
    )
```
